32 devices in a mesh: cp: 8 (over z, x), dp: 4 (over y, core).
Axes of the slice: x: 2, y: 2, z: 4, core: 2. Of those that a mesh axis runs over, the one named last changes fastest.
Arguments:
- queries: bfloat16 [12288, 1024], P('cp', 'dp'), may hold values from -112 to 112, as said below
- keys: bfloat16 [12288, 128], P('cp'), may hold values from -7 to 7
- values: bfloat16 [12288, 128], P('cp'), may hold values from -6 to 6
- out_grad: bfloat16 [12288, 1024], P('cp', 'dp'), may hold values from -6 to 6
- lengths: int32 [24, 4], P('cp'), may hold values from 1 to 509, as said below
- hop_table: int32 [8, 3], P('cp'), may hold values from 0 to 2, each once within a row
Outputs:
- attn_out: bfloat16 [12288, 1024], P('cp', 'dp')
- query_grad: bfloat16 [12288, 1024], P('cp', 'dp')
- key_grad: bfloat16 [12288, 128], P('cp')
- value_grad: bfloat16 [12288, 128], P('cp')
- row_stats: float32 [8, 12288], P('dp', 'cp')
The draws below stay inside these ranges and needn't reach their ends.
Inputs may be any that keep to these rules, and one draw needn't show every extreme that they name: Built so that queries and keys stay within this range. `lengths`: each row sums to 512; every slot of the first quarter of the cp loaders begins with a document of at least 384 rows. `hop_table`: each row names every hop once.
All inputs are finite; a program needn't handle non-finite values.
Results may differ from the reference program's by a relative error of at most 0.006.
Values may be sent and summed in bfloat16 or wider, within the bound.
A program may use at most 128 MiB of HBM per device.

```python
import jax
import jax.numpy as jnp
from jax import lax

HEADS = 8
HD = 128
SLOT = 512
DOCS = 4
HOPS = 3
TOKENS = 12288
N_CP = 8


def query_key_pair(key):
    base_key = jax.random.fold_in(key, 1234)
    key_draw, query_draw = jax.random.split(base_key, 2)
    key_rows = jnp.clip(jax.random.normal(key_draw, (TOKENS, HD), jnp.float32), -6.0, 6.0)
    query_rows = jnp.clip(jax.random.normal(query_draw, (TOKENS, HEADS, HD), jnp.float32), -6.0, 6.0)
    return (query_rows.reshape(TOKENS, HEADS * HD), key_rows)


def draw_queries(key, part):
    return query_key_pair(key)[0].astype(jnp.bfloat16)


def draw_keys(key, part):
    return query_key_pair(key)[1].astype(jnp.bfloat16)


def split_slot(slot_key, long_slot):
    wide_key, narrow_key = jax.random.split(slot_key)
    spread_cuts = jax.random.permutation(wide_key, SLOT - 1)[:DOCS - 1] + 1
    narrow_cuts = jax.random.permutation(narrow_key, SLOT // 4 - 1)[:DOCS - 1] + (SLOT - SLOT // 4 + 1)
    cut_points = jnp.sort(jnp.where(long_slot, narrow_cuts, spread_cuts).astype(jnp.int32))
    boundary = jnp.concatenate([jnp.zeros((1,), jnp.int32), cut_points, jnp.full((1,), SLOT, jnp.int32)])
    return boundary[1:] - boundary[:-1]


def draw_lengths(key, part):
    slot_count = TOKENS // SLOT
    loader_count = slot_count // HOPS
    base_key = jax.random.fold_in(key, 77)
    slot_keys = jax.random.split(base_key, slot_count)
    loader_of = jnp.arange(slot_count, dtype=jnp.int32) // HOPS
    long_slot = loader_of < loader_count // 4
    return jax.vmap(split_slot)(slot_keys, long_slot).astype(jnp.int32)


def block_levels(key, dims, cuts, least, high):
    loudness, own = 1.0, jax.random.fold_in(key, 6)
    for dim, parts in cuts:
        steps = jnp.exp(jax.random.uniform(jax.random.fold_in(own, dim), (parts,), jnp.float32, least / len(cuts), high / len(cuts)))
        loudness = loudness * jnp.repeat(steps, dims[dim] // parts).reshape([-1 if axis == dim else 1 for axis in range(len(dims))])
    return loudness


def scatter_about(rng, dims, deviation, limit, cuts=(), held_as=jnp.bfloat16):
    drawn = deviation * jax.random.normal(rng, dims, jnp.float32)
    if cuts:
        drawn = drawn * block_levels(rng, dims, cuts, -0.22, 0.18)
    return jnp.clip(drawn, -limit, limit).astype(held_as)


def setup_inputs(seed: int = 0) -> dict:
    splits = jax.random.split(jax.random.key(seed), 7)
    queries = draw_queries(jax.random.fold_in(splits[6], 71), 0)
    keys = draw_keys(jax.random.fold_in(splits[6], 71), 0)
    values = scatter_about(splits[2], (TOKENS, HD), 1.0, 6.0, ((0, 8),))
    out_grad = scatter_about(splits[3], (TOKENS, HEADS * HD), 1.0, 6.0, ((0, 8), (1, 4)))
    lengths = draw_lengths(jax.random.fold_in(splits[6], 71), 0)
    hop_table = jax.vmap(lambda own: jax.random.permutation(own, HOPS))(jax.random.split(splits[5], N_CP)).reshape((N_CP, HOPS)).astype(jnp.int32)
    return dict(queries=queries, keys=keys, values=values, out_grad=out_grad, lengths=lengths, hop_table=hop_table)


def segment_rows(doc_lengths, slot_rows):
    doc_ends = jnp.cumsum(doc_lengths)
    position = jnp.arange(slot_rows, dtype=jnp.int32)
    return jnp.sum((position[:, None] >= doc_ends[None, :]).astype(jnp.int32), axis=1)


def slot_pass(queries, keys, values, out_grad, doc_lengths):
    slot_rows = queries.shape[0]
    head_count = queries.shape[1] // HD
    score_scale = HD ** -0.5
    segment = segment_rows(doc_lengths, slot_rows)
    query_heads = queries.astype(jnp.float32).reshape(slot_rows, head_count, HD)
    grad_heads = out_grad.astype(jnp.float32).reshape(slot_rows, head_count, HD)
    key_rows = keys.astype(jnp.float32)
    value_rows = values.astype(jnp.float32)
    position = jnp.arange(slot_rows, dtype=jnp.int32)
    allowed = (segment[:, None] == segment[None, :]) & (position[:, None] >= position[None, :])
    scores = jnp.einsum("shd,td->hst", query_heads, key_rows) * score_scale
    scores = jnp.where(allowed[None], scores, -jnp.inf)
    row_max = jnp.max(scores, axis=2, keepdims=True)
    exp_scores = jnp.exp(scores - row_max)
    row_total = jnp.sum(exp_scores, axis=2, keepdims=True)
    softmax = exp_scores / row_total
    log_total = (row_max + jnp.log(row_total))[:, :, 0]
    weights = softmax.astype(jnp.bfloat16).astype(jnp.float32)
    output = jnp.einsum("hst,td->shd", weights, value_rows)
    row_delta = jnp.sum(grad_heads * output, axis=2)
    prob_grad = jnp.einsum("shd,td->hst", grad_heads, value_rows)
    score_grad = (softmax * (prob_grad - jnp.transpose(row_delta)[:, :, None])).astype(jnp.bfloat16).astype(jnp.float32)
    query_grad = jnp.einsum("hst,td->shd", score_grad, key_rows) * score_scale
    key_grad = jnp.einsum("hst,shd->td", score_grad, query_heads) * score_scale
    value_grad = jnp.einsum("hst,shd->td", weights, grad_heads)
    flat_shape = (slot_rows, head_count * HD)
    return (output.reshape(flat_shape).astype(jnp.bfloat16), query_grad.reshape(flat_shape).astype(jnp.bfloat16),
            key_grad.astype(jnp.bfloat16), value_grad.astype(jnp.bfloat16), log_total)


def run_slot(packed):
    return slot_pass(packed[0], packed[1], packed[2], packed[3], packed[4])


def reference(queries, keys, values, out_grad, lengths, hop_table):
    slot_count = TOKENS // SLOT
    width = HEADS * HD
    results = lax.map(run_slot, (queries.reshape(slot_count, SLOT, width), keys.reshape(slot_count, SLOT, HD),
                                 values.reshape(slot_count, SLOT, HD), out_grad.reshape(slot_count, SLOT, width), lengths))
    attn_out = results[0].reshape(TOKENS, width)
    query_grad = results[1].reshape(TOKENS, width)
    key_grad = results[2].reshape(TOKENS, HD)
    value_grad = results[3].reshape(TOKENS, HD)
    stats = results[4].reshape(N_CP, HOPS, HEADS, SLOT)
    loader_ids = jnp.arange(N_CP, dtype=jnp.int32)
    slot_ids = jnp.arange(HOPS, dtype=jnp.int32)
    gathered = []
    for hop_number in range(HOPS):
        distance = 0 if hop_number == 0 else N_CP >> (HOPS - hop_number)
        source = ((loader_ids - distance) % N_CP).astype(jnp.int32)
        chosen = jnp.sum(jnp.where(hop_table[source] == hop_number, slot_ids[None, :], 0), axis=1).astype(jnp.int32)
        gathered.append(stats[source, chosen])
    owner_stats = jnp.stack(gathered, axis=1)
    row_stats = jnp.transpose(owner_stats, (2, 0, 1, 3)).reshape(HEADS, TOKENS)
    return attn_out, query_grad, key_grad, value_grad, row_stats
```

```python
import functools
import math

import jax
import jax.numpy as jnp
from jax import lax
from jax.experimental import pallas as pl
from jax.experimental.pallas import tpu as pltpu
from jax.sharding import PartitionSpec as P

F32 = jnp.float32
BF16 = jnp.bfloat16
MESH = pl.DeviceIdType.MESH
LOWEST = -1e30


def nt(a, b):
    return lax.dot_general(a, b, (((1,), (1,)), ((), ())), preferred_element_type=F32)


def nn(a, b):
    return lax.dot_general(a, b, (((1,), (0,)), ((), ())), preferred_element_type=F32)


def kernel(
    sizes,
    len_ref,
    hop_ref,
    q_hbm,
    k_hbm,
    v_hbm,
    g_hbm,
    out_ref,
    qg_ref,
    kg_ref,
    vg_ref,
    rs_ref,
    q_v,
    k_v,
    v_v,
    g_v,
    own,
    part,
    precv,
    ysend,
    yrecv,
    fin,
    stats,
    ssend,
    srecv,
    in_sem,
    a_send,
    a_recv,
    b_send,
    b_recv,
    c_send,
    c_recv,
    s_send,
    s_recv,
):
    slots, rows, docs, heads, hd, tiles, cp_count, distances = sizes
    bq = rows // tiles
    half = bq // 2
    scale = hd ** (-0.5)
    c2 = scale * math.log2(math.e)
    cp = lax.axis_index("cp")
    dp = lax.axis_index("dp")
    side = lax.rem(dp, 2)
    outer = dp // 2
    mate = outer * 2 + (1 - side)
    across = (1 - outer) * 2 + side
    barrier = pltpu.get_barrier_semaphore()
    greeted = [{"cp": cp, "dp": mate}, {"cp": cp, "dp": across}]
    for distance in distances:
        greeted.append({"cp": lax.rem(cp + distance, cp_count), "dp": dp})
        greeted.append({"cp": lax.rem(cp + cp_count - distance, cp_count), "dp": dp})
    for target in greeted:
        pl.semaphore_signal(barrier, inc=1, device_id=target, device_id_type=MESH)

    def inputs(s):
        span = pl.ds(s * rows, rows)
        return [
            pltpu.make_async_copy(src.at[span], dst.at[span], in_sem.at[s, n])
            for n, (src, dst) in enumerate(
                ((k_hbm, k_v), (q_hbm, q_v), (v_hbm, v_v), (g_hbm, g_v))
            )
        ]

    for s in range(slots):
        for copy in inputs(s):
            copy.start()

    def to_mate(t):
        return pltpu.make_async_remote_copy(
            src_ref=part.at[t],
            dst_ref=precv.at[t],
            send_sem=a_send.at[t],
            recv_sem=a_recv.at[t],
            device_id={"cp": cp, "dp": mate},
            device_id_type=MESH,
        )

    def to_across(t):
        return pltpu.make_async_remote_copy(
            src_ref=ysend.at[t],
            dst_ref=yrecv.at[t],
            send_sem=b_send.at[t],
            recv_sem=b_recv.at[t],
            device_id={"cp": cp, "dp": across},
            device_id_type=MESH,
        )

    def first_row(t, which):
        s, i = t // tiles, tiles - 1 - t % tiles
        return pl.multiple_of(s * rows + i * bq + which * half, half)

    def shares(t):
        span = pl.ds(first_row(t, side), half)
        return [
            pltpu.make_async_remote_copy(
                src_ref=fin.at[t, n],
                dst_ref=dst.at[span],
                send_sem=c_send.at[t, n],
                recv_sem=c_recv.at[t, n],
                device_id={"cp": cp, "dp": mate},
                device_id_type=MESH,
            )
            for n, dst in enumerate((kg_ref, vg_ref))
        ]

    def stage_b(t):
        to_mate(t).wait_recv()
        ysend[t] = (own[t] + precv[t].astype(F32)).astype(BF16)
        to_across(t).start()

    def stage_c(t):
        to_across(t).wait_recv()
        total = (ysend[t].astype(F32) + yrecv[t].astype(F32)).astype(BF16)
        fin[t] = total
        span = pl.ds(first_row(t, side), half)
        kg_ref[span] = total[0]
        vg_ref[span] = total[1]
        for copy in shares(t):
            copy.start()

    count = slots * tiles
    for s in range(slots):
        for copy in inputs(s):
            copy.wait()
        base = s * rows
        position = lax.broadcasted_iota(jnp.int32, (1, rows), 1)
        start = jnp.zeros((1, rows), jnp.int32)
        end = 0
        for d in range(docs - 1):
            end = end + len_ref[s, d]
            start = jnp.where(position >= end, end, start)
        kt = k_v[base : base + rows].astype(F32).T.astype(BF16)
        vt = v_v[base : base + rows].astype(F32).T.astype(BF16)
        held_k = held_v = None
        for step in range(tiles):
            i = tiles - 1 - step
            t = s * tiles + step
            top = (i + 1) * bq
            k = k_v[base : base + top]
            v = v_v[base : base + top]
            low = i * bq
            key_pos = lax.broadcasted_iota(jnp.int32, (top, bq), 0)
            row_pos = lax.broadcasted_iota(jnp.int32, (top, bq), 1) + low
            allowed = (key_pos >= start[:, low:top]) & (key_pos <= row_pos)
            dk = dv = None
            for h in range(heads):
                lanes = slice(h * hd, (h + 1) * hd)
                q = q_v[base + low : base + top, lanes]
                g = g_v[base + low : base + top, lanes]
                scores = jnp.where(allowed, nt(k, q), LOWEST)
                high = jnp.max(scores, axis=0, keepdims=True)
                e = jnp.exp2((scores - high) * c2)
                total = jnp.sum(e, axis=0, keepdims=True)
                stats[s, h : h + 1, low:top] = high * scale + jnp.log(total)
                p = e * (1.0 / total)
                w = p.astype(BF16)
                pg = nt(v, g)
                delta = jnp.sum(p * pg, axis=0, keepdims=True)
                ds = (p * (pg - delta)).astype(BF16)
                out = nn(vt[:, :top], w)
                out_ref[base + low : base + top, lanes] = out.T.astype(BF16)
                qg = nn(kt[:, :top], ds) * scale
                qg_ref[base + low : base + top, lanes] = qg.T.astype(BF16)
                dv_h = nn(w, g)
                dk_h = nn(ds, q)
                dv = dv_h if dv is None else dv + dv_h
                dk = dk_h if dk is None else dk + dk_h
            if held_k is not None:
                dk = dk + held_k
                dv = dv + held_v
            held_k, held_v = dk[:low], dv[:low]
            dk = dk[low:] * scale
            dv = dv[low:]
            mine_low = side == 0
            own[t, 0] = jnp.where(mine_low, dk[:half], dk[half:])
            own[t, 1] = jnp.where(mine_low, dv[:half], dv[half:])
            part[t, 0] = jnp.where(mine_low, dk[half:], dk[:half]).astype(BF16)
            part[t, 1] = jnp.where(mine_low, dv[half:], dv[:half]).astype(BF16)
            if t == 0:
                pl.semaphore_wait(barrier, len(greeted))
            to_mate(t).start()
            if t >= 1:
                stage_b(t - 1)
            if t >= 3:
                stage_c(t - 3)

    def stat_copy(n):
        return pltpu.make_async_remote_copy(
            src_ref=ssend.at[n],
            dst_ref=srecv.at[n],
            send_sem=s_send.at[n],
            recv_sem=s_recv.at[n],
            device_id={"cp": lax.rem(cp + distances[n], cp_count), "dp": dp},
            device_id_type=MESH,
        )

    for hop in range(slots):
        piece = jnp.zeros((heads, rows), F32)
        for s in range(slots):
            piece = jnp.where(hop_ref[0, s] == hop, stats[s], piece)
        if hop == 0:
            rs_ref[:, 0:rows] = piece
        else:
            ssend[hop - 1] = piece
            stat_copy(hop - 1).start()
    stage_b(count - 1)
    for t in range(max(count - 3, 0), count):
        stage_c(t)
    for n in range(len(distances)):
        stat_copy(n).wait()
        rs_ref[:, (n + 1) * rows : (n + 2) * rows] = srecv[n]
    for t in range(count):
        to_mate(t).wait_send()
        to_across(t).wait_send()
        for copy in shares(t):
            copy.wait()


def local(cp_count, queries, keys, values, out_grad, lengths, hop_table):
    slots, docs = lengths.shape
    rows = queries.shape[0] // slots
    hd = keys.shape[1]
    heads = queries.shape[1] // hd
    tiles = 2
    distances = [cp_count >> (slots - hop) for hop in range(1, slots)]
    count = slots * tiles
    half = rows // tiles // 2
    piece = (count, 2, half, hd)
    sizes = (slots, rows, docs, heads, hd, tiles, cp_count, distances)
    dma = pltpu.SemaphoreType.DMA
    hops = len(distances)
    return tuple(
        pl.pallas_call(
            functools.partial(kernel, sizes),
            name="attend",
            out_shape=[
                jax.ShapeDtypeStruct(queries.shape, BF16),
                jax.ShapeDtypeStruct(queries.shape, BF16),
                jax.ShapeDtypeStruct(keys.shape, BF16),
                jax.ShapeDtypeStruct(values.shape, BF16),
                jax.ShapeDtypeStruct((heads, slots * rows), F32),
            ],
            in_specs=[pl.BlockSpec(memory_space=pltpu.SMEM)] * 2
            + [pl.BlockSpec(memory_space=pl.ANY)] * 4,
            out_specs=[pl.BlockSpec(memory_space=pltpu.VMEM)] * 5,
            scratch_shapes=[
                pltpu.VMEM(queries.shape, BF16),
                pltpu.VMEM(keys.shape, BF16),
                pltpu.VMEM(values.shape, BF16),
                pltpu.VMEM(out_grad.shape, BF16),
                pltpu.VMEM(piece, F32),
                pltpu.VMEM(piece, BF16),
                pltpu.VMEM(piece, BF16),
                pltpu.VMEM(piece, BF16),
                pltpu.VMEM(piece, BF16),
                pltpu.VMEM(piece, BF16),
                pltpu.VMEM((slots, heads, rows), F32),
                pltpu.VMEM((hops, heads, rows), F32),
                pltpu.VMEM((hops, heads, rows), F32),
                dma((slots, 4)),
                dma((count,)),
                dma((count,)),
                dma((count,)),
                dma((count,)),
                dma((count, 2)),
                dma((count, 2)),
                dma((hops,)),
                dma((hops,)),
            ],
            compiler_params=pltpu.CompilerParams(collective_id=0, has_side_effects=True),
        )(lengths, hop_table, queries, keys, values, out_grad)
    )


def solution(mesh):
    return jax.shard_map(
        functools.partial(local, mesh.shape["cp"]),
        mesh=mesh,
        in_specs=(
            P("cp", "dp"),
            P("cp", None),
            P("cp", None),
            P("cp", "dp"),
            P("cp", None),
            P("cp", None),
        ),
        out_specs=(P("cp", "dp"), P("cp", "dp"), P("cp", None), P("cp", None), P("dp", "cp")),
        check_vma=False,
    )
```

```python
import functools
import math

import jax
import jax.numpy as jnp
from jax import lax
from jax.experimental import pallas as pl
from jax.experimental.pallas import tpu as pltpu
from jax.sharding import PartitionSpec as P

F32 = jnp.float32
BF16 = jnp.bfloat16
MESH = pl.DeviceIdType.MESH
LOWEST = -1e30
LAG = 3


def nt(a, b):
    return lax.dot_general(a, b, (((1,), (1,)), ((), ())), preferred_element_type=F32)


def nn(a, b):
    return lax.dot_general(a, b, (((1,), (0,)), ((), ())), preferred_element_type=F32)


def kernel(
    sizes,
    len_ref,
    hop_ref,
    q_hbm,
    k_hbm,
    v_hbm,
    g_hbm,
    out_ref,
    qg_ref,
    kg_ref,
    vg_ref,
    rs_ref,
    q_v,
    k_v,
    v_v,
    g_v,
    own,
    part,
    precv,
    ysend,
    yrecv,
    fin,
    stats,
    ssend,
    srecv,
    in_sem,
    a_send,
    a_recv,
    b_send,
    b_recv,
    c_send,
    c_recv,
    s_send,
    s_recv,
):
    slots, rows, docs, heads, hd, tiles, cp_count, distances = sizes
    bq = rows // tiles
    half = bq // 2
    scale = hd ** (-0.5)
    c2 = scale * math.log2(math.e)
    cp = lax.axis_index("cp")
    dp = lax.axis_index("dp")
    side = lax.rem(dp, 2)
    outer = dp // 2
    mate = outer * 2 + (1 - side)
    across = (1 - outer) * 2 + side
    barrier = pltpu.get_barrier_semaphore()
    greeted = [{"cp": cp, "dp": mate}, {"cp": cp, "dp": across}]
    for distance in distances:
        greeted.append({"cp": lax.rem(cp + distance, cp_count), "dp": dp})
        greeted.append({"cp": lax.rem(cp + cp_count - distance, cp_count), "dp": dp})
    for target in greeted:
        pl.semaphore_signal(barrier, inc=1, device_id=target, device_id_type=MESH)

    def inputs(s):
        span = pl.ds(s * rows, rows)
        return [
            pltpu.make_async_copy(src.at[span], dst.at[span], in_sem.at[s, n])
            for n, (src, dst) in enumerate(
                ((k_hbm, k_v), (q_hbm, q_v), (v_hbm, v_v), (g_hbm, g_v))
            )
        ]

    for s in range(slots):
        for copy in inputs(s):
            copy.start()

    def to_mate(t):
        return pltpu.make_async_remote_copy(
            src_ref=part.at[t],
            dst_ref=precv.at[t],
            send_sem=a_send.at[t],
            recv_sem=a_recv.at[t],
            device_id={"cp": cp, "dp": mate},
            device_id_type=MESH,
        )

    def to_across(t):
        return pltpu.make_async_remote_copy(
            src_ref=ysend.at[t],
            dst_ref=yrecv.at[t],
            send_sem=b_send.at[t],
            recv_sem=b_recv.at[t],
            device_id={"cp": cp, "dp": across},
            device_id_type=MESH,
        )

    def first_row(t, which):
        s, i = t // tiles, tiles - 1 - t % tiles
        return pl.multiple_of(s * rows + i * bq + which * half, half)

    def shares(t):
        span = pl.ds(first_row(t, side), half)
        return [
            pltpu.make_async_remote_copy(
                src_ref=fin.at[t, n],
                dst_ref=dst.at[span],
                send_sem=c_send.at[t, n],
                recv_sem=c_recv.at[t, n],
                device_id={"cp": cp, "dp": mate},
                device_id_type=MESH,
            )
            for n, dst in enumerate((kg_ref, vg_ref))
        ]

    def stage_b(t):
        to_mate(t).wait_recv()
        ysend[t] = (own[t] + precv[t].astype(F32)).astype(BF16)
        to_across(t).start()

    def stage_c(t):
        to_across(t).wait_recv()
        total = (ysend[t].astype(F32) + yrecv[t].astype(F32)).astype(BF16)
        fin[t] = total
        span = pl.ds(first_row(t, side), half)
        kg_ref[span] = total[0]
        vg_ref[span] = total[1]
        for copy in shares(t):
            copy.start()

    pending = []

    def finish(left):
        while len(pending) > left * heads:
            span, lanes, vt, kt, w, ds = pending.pop(0)
            out_ref[span, lanes] = nn(vt, w).T.astype(BF16)
            qg_ref[span, lanes] = (nn(kt, ds) * scale).T.astype(BF16)

    count = slots * tiles
    for s in range(slots):
        for copy in inputs(s):
            copy.wait()
        base = s * rows
        position = lax.broadcasted_iota(jnp.int32, (1, rows), 1)
        start = jnp.zeros((1, rows), jnp.int32)
        end = 0
        for d in range(docs - 1):
            end = end + len_ref[s, d]
            start = jnp.where(position >= end, end, start)
        kt = k_v[base : base + rows].astype(F32).T.astype(BF16)
        vt = v_v[base : base + rows].astype(F32).T.astype(BF16)
        held_k = held_v = None
        for step in range(tiles):
            i = tiles - 1 - step
            t = s * tiles + step
            top = (i + 1) * bq
            k = k_v[base : base + top]
            v = v_v[base : base + top]
            low = i * bq
            key_pos = lax.broadcasted_iota(jnp.int32, (top, bq), 0)
            row_pos = lax.broadcasted_iota(jnp.int32, (top, bq), 1) + low
            allowed = (key_pos >= start[:, low:top]) & (key_pos <= row_pos)
            dk = dv = None
            for h in range(heads):
                lanes = slice(h * hd, (h + 1) * hd)
                q = q_v[base + low : base + top, lanes]
                g = g_v[base + low : base + top, lanes]
                scores = jnp.where(allowed, nt(k, q), LOWEST)
                high = jnp.max(scores, axis=0, keepdims=True)
                e = jnp.exp2((scores - high) * c2)
                total = jnp.sum(e, axis=0, keepdims=True)
                stats[s, h : h + 1, low:top] = high * scale + jnp.log(total)
                p = e * (1.0 / total)
                w = p.astype(BF16)
                pg = nt(v, g)
                delta = jnp.sum(p * pg, axis=0, keepdims=True)
                ds = (p * (pg - delta)).astype(BF16)
                dv_h = nn(w, g)
                dk_h = nn(ds, q)
                dv = dv_h if dv is None else dv + dv_h
                dk = dk_h if dk is None else dk + dk_h
                span = slice(base + low, base + top)
                pending.append((span, lanes, vt[:, :top], kt[:, :top], w, ds))
            if held_k is not None:
                dk = dk + held_k
                dv = dv + held_v
            held_k, held_v = dk[:low], dv[:low]
            dk = dk[low:] * scale
            dv = dv[low:]
            mine_low = side == 0
            own[t, 0] = jnp.where(mine_low, dk[:half], dk[half:])
            own[t, 1] = jnp.where(mine_low, dv[:half], dv[half:])
            part[t, 0] = jnp.where(mine_low, dk[half:], dk[:half]).astype(BF16)
            part[t, 1] = jnp.where(mine_low, dv[half:], dv[:half]).astype(BF16)
            if t == 0:
                pl.semaphore_wait(barrier, len(greeted))
            to_mate(t).start()
            finish(LAG)
            if t >= 1:
                stage_b(t - 1)
            if t >= 3:
                stage_c(t - 3)

    def stat_copy(n):
        return pltpu.make_async_remote_copy(
            src_ref=ssend.at[n],
            dst_ref=srecv.at[n],
            send_sem=s_send.at[n],
            recv_sem=s_recv.at[n],
            device_id={"cp": lax.rem(cp + distances[n], cp_count), "dp": dp},
            device_id_type=MESH,
        )

    for hop in range(slots):
        piece = jnp.zeros((heads, rows), F32)
        for s in range(slots):
            piece = jnp.where(hop_ref[0, s] == hop, stats[s], piece)
        if hop == 0:
            rs_ref[:, 0:rows] = piece
        else:
            ssend[hop - 1] = piece
            stat_copy(hop - 1).start()
    stage_b(count - 1)
    finish(0)
    for t in range(max(count - 3, 0), count):
        stage_c(t)
    for n in range(len(distances)):
        stat_copy(n).wait()
        rs_ref[:, (n + 1) * rows : (n + 2) * rows] = srecv[n]
    for t in range(count):
        to_mate(t).wait_send()
        to_across(t).wait_send()
        for copy in shares(t):
            copy.wait()


def flush(*refs):
    sem = refs[-1]
    count = len(refs) // 2
    copies = [
        pltpu.make_async_copy(refs[n], refs[count + n], sem.at[n]) for n in range(count)
    ]
    for copy in copies:
        copy.start()
    for copy in copies:
        copy.wait()


def local(cp_count, queries, keys, values, out_grad, lengths, hop_table):
    slots, docs = lengths.shape
    rows = queries.shape[0] // slots
    hd = keys.shape[1]
    heads = queries.shape[1] // hd
    tiles = 2
    distances = [cp_count >> (slots - hop) for hop in range(1, slots)]
    count = slots * tiles
    half = rows // tiles // 2
    piece = (count, 2, half, hd)
    sizes = (slots, rows, docs, heads, hd, tiles, cp_count, distances)
    dma = pltpu.SemaphoreType.DMA
    hops = len(distances)
    results = [
        (queries.shape, BF16),
        (queries.shape, BF16),
        (keys.shape, BF16),
        (values.shape, BF16),
        ((heads, slots * rows), F32),
    ]
    held = pl.pallas_call(
        functools.partial(kernel, sizes),
        name="attend",
        out_shape=[pltpu.VMEM(*result) for result in results],
        in_specs=[pl.BlockSpec(memory_space=pltpu.SMEM)] * 2
        + [pl.BlockSpec(memory_space=pl.ANY)] * 4,
        out_specs=[pl.BlockSpec(memory_space=pltpu.VMEM)] * 5,
        scratch_shapes=[
            pltpu.VMEM(queries.shape, BF16),
            pltpu.VMEM(keys.shape, BF16),
            pltpu.VMEM(values.shape, BF16),
            pltpu.VMEM(out_grad.shape, BF16),
            pltpu.VMEM(piece, F32),
            pltpu.VMEM(piece, BF16),
            pltpu.VMEM(piece, BF16),
            pltpu.VMEM(piece, BF16),
            pltpu.VMEM(piece, BF16),
            pltpu.VMEM(piece, BF16),
            pltpu.VMEM((slots, heads, rows), F32),
            pltpu.VMEM((hops, heads, rows), F32),
            pltpu.VMEM((hops, heads, rows), F32),
            dma((slots, 4)),
            dma((count,)),
            dma((count,)),
            dma((count,)),
            dma((count,)),
            dma((count, 2)),
            dma((count, 2)),
            dma((hops,)),
            dma((hops,)),
        ],
        compiler_params=pltpu.CompilerParams(collective_id=0, has_side_effects=True),
    )(lengths, hop_table, queries, keys, values, out_grad)
    return tuple(
        pl.pallas_call(
            flush,
            name="flush",
            out_shape=[jax.ShapeDtypeStruct(*result) for result in results],
            in_specs=[pl.BlockSpec(memory_space=pltpu.VMEM)] * 5,
            out_specs=[pl.BlockSpec(memory_space=pl.ANY)] * 5,
            scratch_shapes=[dma((5,))],
        )(*[pltpu.with_memory_space_constraint(x, pltpu.VMEM) for x in held])
    )


def solution(mesh):
    return jax.shard_map(
        functools.partial(local, mesh.shape["cp"]),
        mesh=mesh,
        in_specs=(
            P("cp", "dp"),
            P("cp", None),
            P("cp", None),
            P("cp", "dp"),
            P("cp", None),
            P("cp", None),
        ),
        out_specs=(P("cp", "dp"), P("cp", "dp"), P("cp", None), P("cp", None), P("dp", "cp")),
        check_vma=False,
    )
```

```python
import functools
import math

import jax
import jax.numpy as jnp
from jax import lax
from jax.experimental import pallas as pl
from jax.experimental.pallas import tpu as pltpu
from jax.sharding import PartitionSpec as P

F32 = jnp.float32
BF16 = jnp.bfloat16
MESH = pl.DeviceIdType.MESH
LOWEST = -1e30
FINISH_LAG = 6
PAIR_LAG = 2
SHARE_LAG = 6


def nt(a, b):
    return lax.dot_general(a, b, (((1,), (1,)), ((), ())), preferred_element_type=F32)


def nn(a, b):
    return lax.dot_general(a, b, (((1,), (0,)), ((), ())), preferred_element_type=F32)


def kernel(
    sizes,
    len_ref,
    hop_ref,
    q_hbm,
    k_hbm,
    v_hbm,
    g_hbm,
    out_ref,
    qg_ref,
    kg_ref,
    vg_ref,
    rs_ref,
    q_v,
    k_v,
    v_v,
    g_v,
    own,
    part,
    precv,
    ysend,
    yrecv,
    fin,
    stats,
    ssend,
    srecv,
    in_sem,
    a_send,
    a_recv,
    b_send,
    b_recv,
    c_send,
    c_recv,
    s_send,
    s_recv,
):
    slots, rows, docs, heads, hd, tiles, cp_count, distances = sizes
    bq = rows // tiles
    half = bq // 2
    scale = hd ** (-0.5)
    c2 = scale * math.log2(math.e)
    cp = lax.axis_index("cp")
    dp = lax.axis_index("dp")
    side = lax.rem(dp, 2)
    outer = dp // 2
    mate = outer * 2 + (1 - side)
    across = (1 - outer) * 2 + side
    barrier = pltpu.get_barrier_semaphore()
    greeted = [{"cp": cp, "dp": mate}, {"cp": cp, "dp": across}]
    for distance in distances:
        greeted.append({"cp": lax.rem(cp + distance, cp_count), "dp": dp})
        greeted.append({"cp": lax.rem(cp + cp_count - distance, cp_count), "dp": dp})
    for target in greeted:
        pl.semaphore_signal(barrier, inc=1, device_id=target, device_id_type=MESH)

    def inputs(s):
        span = pl.ds(s * rows, rows)
        return [
            pltpu.make_async_copy(src.at[span], dst.at[span], in_sem.at[s, n])
            for n, (src, dst) in enumerate(
                ((k_hbm, k_v), (q_hbm, q_v), (v_hbm, v_v), (g_hbm, g_v))
            )
        ]

    for copy in inputs(0):
        copy.start()

    def to_mate(t):
        return pltpu.make_async_remote_copy(
            src_ref=part.at[t],
            dst_ref=precv.at[t],
            send_sem=a_send.at[t],
            recv_sem=a_recv.at[t],
            device_id={"cp": cp, "dp": mate},
            device_id_type=MESH,
        )

    def to_across(t):
        return pltpu.make_async_remote_copy(
            src_ref=ysend.at[t],
            dst_ref=yrecv.at[t],
            send_sem=b_send.at[t],
            recv_sem=b_recv.at[t],
            device_id={"cp": cp, "dp": across},
            device_id_type=MESH,
        )

    def first_row(t, which):
        s, i = t // tiles, tiles - 1 - t % tiles
        return pl.multiple_of(s * rows + i * bq + which * half, half)

    def shares(t):
        span = pl.ds(first_row(t, side), half)
        return [
            pltpu.make_async_remote_copy(
                src_ref=fin.at[t, n],
                dst_ref=dst.at[span],
                send_sem=c_send.at[t, n],
                recv_sem=c_recv.at[t, n],
                device_id={"cp": cp, "dp": mate},
                device_id_type=MESH,
            )
            for n, dst in enumerate((kg_ref, vg_ref))
        ]

    def stage_b(t):
        to_mate(t).wait_recv()
        ysend[t] = (own[t] + precv[t].astype(F32)).astype(BF16)
        to_across(t).start()

    def stage_c(t):
        to_across(t).wait_recv()
        total = (ysend[t].astype(F32) + yrecv[t].astype(F32)).astype(BF16)
        fin[t] = total
        span = pl.ds(first_row(t, side), half)
        kg_ref[span] = total[0]
        vg_ref[span] = total[1]
        for copy in shares(t):
            copy.start()

    pending = []

    def side_by_side(ref, span):
        return jnp.concatenate(
            [ref[span, h * hd : (h + 1) * hd] for h in range(heads)], axis=0
        )

    def finish(left):
        while len(pending) > left:
            span, vt, kt, w, ds = pending.pop(0)
            out = nn(vt, w).T.astype(BF16)
            qg = (nn(kt, ds) * scale).T.astype(BF16)
            for h in range(heads):
                out_ref[span, h * hd : (h + 1) * hd] = out[h * bq : (h + 1) * bq]
                qg_ref[span, h * hd : (h + 1) * hd] = qg[h * bq : (h + 1) * bq]

    count = slots * tiles
    for s in range(slots):
        for copy in inputs(s):
            copy.wait()
        if s == 0:
            for later in range(1, slots):
                for copy in inputs(later):
                    copy.start()
        base = s * rows
        position = lax.broadcasted_iota(jnp.int32, (1, rows), 1)
        start = jnp.zeros((1, rows), jnp.int32)
        end = 0
        for d in range(docs - 1):
            end = end + len_ref[s, d]
            start = jnp.where(position >= end, end, start)
        kt = k_v[base : base + rows].astype(F32).T.astype(BF16)
        vt = v_v[base : base + rows].astype(F32).T.astype(BF16)
        held_k = held_v = None
        for step in range(tiles):
            i = tiles - 1 - step
            t = s * tiles + step
            top = (i + 1) * bq
            k = k_v[base : base + top]
            v = v_v[base : base + top]
            low = i * bq
            key_pos = lax.broadcasted_iota(jnp.int32, (top, bq), 0)
            row_pos = lax.broadcasted_iota(jnp.int32, (top, bq), 1) + low
            allowed = (key_pos >= start[:, low:top]) & (key_pos <= row_pos)
            span = slice(base + low, base + top)
            q = side_by_side(q_v, span)
            g = side_by_side(g_v, span)
            raw = nt(k, q)
            scores = jnp.concatenate(
                [
                    jnp.where(allowed, raw[:, h * bq : (h + 1) * bq], LOWEST)
                    for h in range(heads)
                ],
                axis=1,
            )
            high = jnp.max(scores, axis=0, keepdims=True)
            e = jnp.exp2((scores - high) * c2)
            total = jnp.sum(e, axis=0, keepdims=True)
            stat = high * scale + jnp.log(total)
            for h in range(heads):
                stats[s, h : h + 1, low:top] = stat[:, h * bq : (h + 1) * bq]
            p = e * (1.0 / total)
            w = p.astype(BF16)
            pg = nt(v, g)
            delta = jnp.sum(p * pg, axis=0, keepdims=True)
            ds = (p * (pg - delta)).astype(BF16)
            dv = nn(w, g)
            dk = nn(ds, q)
            pending.append((span, vt[:, :top], kt[:, :top], w, ds))
            if held_k is not None:
                dk = dk + held_k
                dv = dv + held_v
            held_k, held_v = dk[:low], dv[:low]
            dk = dk[low:] * scale
            dv = dv[low:]
            mine_low = side == 0
            own[t, 0] = jnp.where(mine_low, dk[:half], dk[half:])
            own[t, 1] = jnp.where(mine_low, dv[:half], dv[half:])
            part[t, 0] = jnp.where(mine_low, dk[half:], dk[:half]).astype(BF16)
            part[t, 1] = jnp.where(mine_low, dv[half:], dv[:half]).astype(BF16)
            if t == 0:
                pl.semaphore_wait(barrier, len(greeted))
            to_mate(t).start()
            if t >= PAIR_LAG:
                stage_b(t - PAIR_LAG)
            finish(FINISH_LAG)
            if t >= SHARE_LAG:
                stage_c(t - SHARE_LAG)

    def stat_copy(n):
        return pltpu.make_async_remote_copy(
            src_ref=ssend.at[n],
            dst_ref=srecv.at[n],
            send_sem=s_send.at[n],
            recv_sem=s_recv.at[n],
            device_id={"cp": lax.rem(cp + distances[n], cp_count), "dp": dp},
            device_id_type=MESH,
        )

    for hop in range(slots):
        piece = jnp.zeros((heads, rows), F32)
        for s in range(slots):
            piece = jnp.where(hop_ref[0, s] == hop, stats[s], piece)
        if hop == 0:
            rs_ref[:, 0:rows] = piece
        else:
            ssend[hop - 1] = piece
            stat_copy(hop - 1).start()
    for t in range(count - PAIR_LAG, count):
        finish(FINISH_LAG - 1 - (t - count + PAIR_LAG))
        stage_b(t)
    finish(0)
    for t in range(count - SHARE_LAG, count):
        stage_c(t)
    for n in range(len(distances)):
        stat_copy(n).wait()
        rs_ref[:, (n + 1) * rows : (n + 2) * rows] = srecv[n]
    for t in range(count):
        to_mate(t).wait_send()
        to_across(t).wait_send()
        for copy in shares(t):
            copy.wait()


def flush(*refs):
    sem = refs[-1]
    count = len(refs) // 2
    copies = [
        pltpu.make_async_copy(refs[n], refs[count + n], sem.at[n]) for n in range(count)
    ]
    for copy in copies:
        copy.start()
    for copy in copies:
        copy.wait()


def local(cp_count, queries, keys, values, out_grad, lengths, hop_table):
    slots, docs = lengths.shape
    rows = queries.shape[0] // slots
    hd = keys.shape[1]
    heads = queries.shape[1] // hd
    tiles = 4
    distances = [cp_count >> (slots - hop) for hop in range(1, slots)]
    count = slots * tiles
    half = rows // tiles // 2
    piece = (count, 2, half, hd)
    sizes = (slots, rows, docs, heads, hd, tiles, cp_count, distances)
    dma = pltpu.SemaphoreType.DMA
    hops = len(distances)
    results = [
        (queries.shape, BF16),
        (queries.shape, BF16),
        (keys.shape, BF16),
        (values.shape, BF16),
        ((heads, slots * rows), F32),
    ]
    held = pl.pallas_call(
        functools.partial(kernel, sizes),
        name="attend",
        out_shape=[pltpu.VMEM(*result) for result in results],
        in_specs=[pl.BlockSpec(memory_space=pltpu.SMEM)] * 2
        + [pl.BlockSpec(memory_space=pl.ANY)] * 4,
        out_specs=[pl.BlockSpec(memory_space=pltpu.VMEM)] * 5,
        scratch_shapes=[
            pltpu.VMEM(queries.shape, BF16),
            pltpu.VMEM(keys.shape, BF16),
            pltpu.VMEM(values.shape, BF16),
            pltpu.VMEM(out_grad.shape, BF16),
            pltpu.VMEM(piece, F32),
            pltpu.VMEM(piece, BF16),
            pltpu.VMEM(piece, BF16),
            pltpu.VMEM(piece, BF16),
            pltpu.VMEM(piece, BF16),
            pltpu.VMEM(piece, BF16),
            pltpu.VMEM((slots, heads, rows), F32),
            pltpu.VMEM((hops, heads, rows), F32),
            pltpu.VMEM((hops, heads, rows), F32),
            dma((slots, 4)),
            dma((count,)),
            dma((count,)),
            dma((count,)),
            dma((count,)),
            dma((count, 2)),
            dma((count, 2)),
            dma((hops,)),
            dma((hops,)),
        ],
        compiler_params=pltpu.CompilerParams(collective_id=0, has_side_effects=True),
    )(lengths, hop_table, queries, keys, values, out_grad)
    return tuple(
        pl.pallas_call(
            flush,
            name="flush",
            out_shape=[jax.ShapeDtypeStruct(*result) for result in results],
            in_specs=[pl.BlockSpec(memory_space=pltpu.VMEM)] * 5,
            out_specs=[pl.BlockSpec(memory_space=pl.ANY)] * 5,
            scratch_shapes=[dma((5,))],
        )(*[pltpu.with_memory_space_constraint(x, pltpu.VMEM) for x in held])
    )


def solution(mesh):
    return jax.shard_map(
        functools.partial(local, mesh.shape["cp"]),
        mesh=mesh,
        in_specs=(
            P("cp", "dp"),
            P("cp", None),
            P("cp", None),
            P("cp", "dp"),
            P("cp", None),
            P("cp", None),
        ),
        out_specs=(P("cp", "dp"), P("cp", "dp"), P("cp", None), P("cp", None), P("dp", "cp")),
        check_vma=False,
    )
```

```python
import functools
import math

import jax
import jax.numpy as jnp
from jax import lax
from jax.experimental import pallas as pl
from jax.experimental.pallas import tpu as pltpu
from jax.sharding import PartitionSpec as P

F32 = jnp.float32
BF16 = jnp.bfloat16
MESH = pl.DeviceIdType.MESH
LOWEST = -1e30
LAG = 3


def nt(a, b):
    return lax.dot_general(a, b, (((1,), (1,)), ((), ())), preferred_element_type=F32)


def nn(a, b):
    return lax.dot_general(a, b, (((1,), (0,)), ((), ())), preferred_element_type=F32)


def kernel(
    sizes,
    len_hbm,
    hop_hbm,
    q_hbm,
    k_hbm,
    v_hbm,
    g_hbm,
    out_ref,
    qg_ref,
    kg_ref,
    vg_ref,
    rs_ref,
    len_ref,
    hop_ref,
    q_v,
    k_v,
    v_v,
    g_v,
    own,
    part,
    precv,
    ysend,
    yrecv,
    fin,
    stats,
    ssend,
    srecv,
    in_sem,
    table_sem,
    a_send,
    a_recv,
    b_send,
    b_recv,
    c_send,
    c_recv,
    s_send,
    s_recv,
):
    slots, rows, docs, heads, hd, tiles, cp_count, distances = sizes
    bq = rows // tiles
    half = bq // 2
    scale = hd ** (-0.5)
    c2 = scale * math.log2(math.e)
    cp = lax.axis_index("cp")
    dp = lax.axis_index("dp")
    side = lax.rem(dp, 2)
    outer = dp // 2
    mate = outer * 2 + (1 - side)
    across = (1 - outer) * 2 + side
    barrier = pltpu.get_barrier_semaphore()
    greeted = []
    for distance in reversed(distances):
        greeted.append({"cp": lax.rem(cp + distance, cp_count), "dp": dp})
        greeted.append({"cp": lax.rem(cp + cp_count - distance, cp_count), "dp": dp})
    greeted += [{"cp": cp, "dp": across}, {"cp": cp, "dp": mate}]
    for target in greeted:
        pl.semaphore_signal(barrier, inc=1, device_id=target, device_id_type=MESH)

    def inputs(s):
        span = pl.ds(s * rows, rows)
        return [
            pltpu.make_async_copy(src.at[span], dst.at[span], in_sem.at[s, n])
            for n, (src, dst) in enumerate(
                ((k_hbm, k_v), (q_hbm, q_v), (v_hbm, v_v), (g_hbm, g_v))
            )
        ]

    tables = [
        pltpu.make_async_copy(len_hbm, len_ref, table_sem.at[0]),
        pltpu.make_async_copy(hop_hbm, hop_ref, table_sem.at[1]),
    ]
    for copy in tables + inputs(0):
        copy.start()
    for copy in tables:
        copy.wait()

    def to_mate(t):
        return pltpu.make_async_remote_copy(
            src_ref=part.at[t],
            dst_ref=precv.at[t],
            send_sem=a_send.at[t],
            recv_sem=a_recv.at[t],
            device_id={"cp": cp, "dp": mate},
            device_id_type=MESH,
        )

    def to_across(t):
        return pltpu.make_async_remote_copy(
            src_ref=ysend.at[t],
            dst_ref=yrecv.at[t],
            send_sem=b_send.at[t],
            recv_sem=b_recv.at[t],
            device_id={"cp": cp, "dp": across},
            device_id_type=MESH,
        )

    def first_row(t, which):
        s, i = t // tiles, tiles - 1 - t % tiles
        return pl.multiple_of(s * rows + i * bq + which * half, half)

    def shares(t):
        span = pl.ds(first_row(t, side), half)
        return [
            pltpu.make_async_remote_copy(
                src_ref=fin.at[t, n],
                dst_ref=dst.at[span],
                send_sem=c_send.at[t, n],
                recv_sem=c_recv.at[t, n],
                device_id={"cp": cp, "dp": mate},
                device_id_type=MESH,
            )
            for n, dst in enumerate((kg_ref, vg_ref))
        ]

    def stage_b(t):
        to_mate(t).wait_recv()
        ysend[t] = (own[t] + precv[t].astype(F32)).astype(BF16)
        to_across(t).start()

    def stage_c(t):
        to_across(t).wait_recv()
        total = (ysend[t].astype(F32) + yrecv[t].astype(F32)).astype(BF16)
        fin[t] = total
        span = pl.ds(first_row(t, side), half)
        kg_ref[span] = total[0]
        vg_ref[span] = total[1]
        for copy in shares(t):
            copy.start()

    pending = []

    def finish(left):
        while len(pending) > left * heads:
            span, lanes, vt, kt, w, ds = pending.pop(0)
            out_ref[span, lanes] = nn(vt, w).T.astype(BF16)
            qg_ref[span, lanes] = (nn(kt, ds) * scale).T.astype(BF16)

    count = slots * tiles
    for s in range(slots):
        for copy in inputs(s):
            copy.wait()
        if s == 0:
            for later in range(1, slots):
                for copy in inputs(later):
                    copy.start()
        base = s * rows
        position = lax.broadcasted_iota(jnp.int32, (1, rows), 1)
        start = jnp.zeros((1, rows), jnp.int32)
        end = 0
        for d in range(docs - 1):
            end = end + len_ref[s, d]
            start = jnp.where(position >= end, end, start)
        kt = k_v[base : base + rows].astype(F32).T.astype(BF16)
        vt = v_v[base : base + rows].astype(F32).T.astype(BF16)
        held_k = held_v = None
        for step in range(tiles):
            i = tiles - 1 - step
            t = s * tiles + step
            top = (i + 1) * bq
            k = k_v[base : base + top]
            v = v_v[base : base + top]
            low = i * bq
            key_pos = lax.broadcasted_iota(jnp.int32, (top, bq), 0)
            row_pos = lax.broadcasted_iota(jnp.int32, (top, bq), 1) + low
            allowed = (key_pos >= start[:, low:top]) & (key_pos <= row_pos)
            dk = dv = None
            for h in range(heads):
                lanes = slice(h * hd, (h + 1) * hd)
                q = q_v[base + low : base + top, lanes]
                g = g_v[base + low : base + top, lanes]
                scores = jnp.where(allowed, nt(k, q), LOWEST)
                high = jnp.max(scores, axis=0, keepdims=True)
                e = jnp.exp2((scores - high) * c2)
                total = jnp.sum(e, axis=0, keepdims=True)
                stats[s, h : h + 1, low:top] = high * scale + jnp.log(total)
                p = e * (1.0 / total)
                w = p.astype(BF16)
                pg = nt(v, g)
                delta = jnp.sum(p * pg, axis=0, keepdims=True)
                ds = (p * (pg - delta)).astype(BF16)
                dv_h = nn(w, g)
                dk_h = nn(ds, q)
                dv = dv_h if dv is None else dv + dv_h
                dk = dk_h if dk is None else dk + dk_h
                span = slice(base + low, base + top)
                pending.append((span, lanes, vt[:, :top], kt[:, :top], w, ds))
            if held_k is not None:
                dk = dk + held_k
                dv = dv + held_v
            held_k, held_v = dk[:low], dv[:low]
            dk = dk[low:] * scale
            dv = dv[low:]
            mine_low = side == 0
            own[t, 0] = jnp.where(mine_low, dk[:half], dk[half:])
            own[t, 1] = jnp.where(mine_low, dv[:half], dv[half:])
            part[t, 0] = jnp.where(mine_low, dk[half:], dk[:half]).astype(BF16)
            part[t, 1] = jnp.where(mine_low, dv[half:], dv[:half]).astype(BF16)
            if t == 0:
                pl.semaphore_wait(barrier, len(greeted))
            to_mate(t).start()
            finish(LAG)
            if t >= 1:
                stage_b(t - 1)
            if t >= 3:
                stage_c(t - 3)

    def stat_copy(n):
        return pltpu.make_async_remote_copy(
            src_ref=ssend.at[n],
            dst_ref=srecv.at[n],
            send_sem=s_send.at[n],
            recv_sem=s_recv.at[n],
            device_id={"cp": lax.rem(cp + distances[n], cp_count), "dp": dp},
            device_id_type=MESH,
        )

    for hop in range(slots):
        piece = jnp.zeros((heads, rows), F32)
        for s in range(slots):
            piece = jnp.where(hop_ref[0, s] == hop, stats[s], piece)
        if hop == 0:
            rs_ref[:, 0:rows] = piece
        else:
            ssend[hop - 1] = piece
            stat_copy(hop - 1).start()
    stage_b(count - 1)
    finish(0)
    for t in range(max(count - 3, 0), count):
        stage_c(t)
    for n in range(len(distances)):
        stat_copy(n).wait()
        rs_ref[:, (n + 1) * rows : (n + 2) * rows] = srecv[n]
    for t in range(count):
        to_mate(t).wait_send()
        to_across(t).wait_send()
        for copy in shares(t):
            copy.wait()


def flush(*refs):
    sem = refs[-1]
    count = len(refs) // 2
    copies = [
        pltpu.make_async_copy(refs[n], refs[count + n], sem.at[n]) for n in range(count)
    ]
    for copy in copies:
        copy.start()
    for copy in copies:
        copy.wait()


def local(cp_count, queries, keys, values, out_grad, lengths, hop_table):
    slots, docs = lengths.shape
    rows = queries.shape[0] // slots
    hd = keys.shape[1]
    heads = queries.shape[1] // hd
    tiles = 2
    distances = [cp_count >> (slots - hop) for hop in range(1, slots)]
    count = slots * tiles
    half = rows // tiles // 2
    piece = (count, 2, half, hd)
    sizes = (slots, rows, docs, heads, hd, tiles, cp_count, distances)
    dma = pltpu.SemaphoreType.DMA
    hops = len(distances)
    results = [
        (queries.shape, BF16),
        (queries.shape, BF16),
        (keys.shape, BF16),
        (values.shape, BF16),
        ((heads, slots * rows), F32),
    ]
    held = pl.pallas_call(
        functools.partial(kernel, sizes),
        name="attend",
        out_shape=[pltpu.VMEM(*result) for result in results],
        in_specs=[pl.BlockSpec(memory_space=pl.ANY)] * 6,
        out_specs=[pl.BlockSpec(memory_space=pltpu.VMEM)] * 5,
        scratch_shapes=[
            pltpu.SMEM(lengths.shape, jnp.int32),
            pltpu.SMEM(hop_table.shape, jnp.int32),
            pltpu.VMEM(queries.shape, BF16),
            pltpu.VMEM(keys.shape, BF16),
            pltpu.VMEM(values.shape, BF16),
            pltpu.VMEM(out_grad.shape, BF16),
            pltpu.VMEM(piece, F32),
            pltpu.VMEM(piece, BF16),
            pltpu.VMEM(piece, BF16),
            pltpu.VMEM(piece, BF16),
            pltpu.VMEM(piece, BF16),
            pltpu.VMEM(piece, BF16),
            pltpu.VMEM((slots, heads, rows), F32),
            pltpu.VMEM((hops, heads, rows), F32),
            pltpu.VMEM((hops, heads, rows), F32),
            dma((slots, 4)),
            dma((2,)),
            dma((count,)),
            dma((count,)),
            dma((count,)),
            dma((count,)),
            dma((count, 2)),
            dma((count, 2)),
            dma((hops,)),
            dma((hops,)),
        ],
        compiler_params=pltpu.CompilerParams(collective_id=0, has_side_effects=True),
    )(lengths, hop_table, queries, keys, values, out_grad)
    return tuple(
        pl.pallas_call(
            flush,
            name="flush",
            out_shape=[jax.ShapeDtypeStruct(*result) for result in results],
            in_specs=[pl.BlockSpec(memory_space=pltpu.VMEM)] * 5,
            out_specs=[pl.BlockSpec(memory_space=pl.ANY)] * 5,
            scratch_shapes=[dma((5,))],
        )(*[pltpu.with_memory_space_constraint(x, pltpu.VMEM) for x in held])
    )


def solution(mesh):
    return jax.shard_map(
        functools.partial(local, mesh.shape["cp"]),
        mesh=mesh,
        in_specs=(
            P("cp", "dp"),
            P("cp", None),
            P("cp", None),
            P("cp", "dp"),
            P("cp", None),
            P("cp", None),
        ),
        out_specs=(P("cp", "dp"), P("cp", "dp"), P("cp", None), P("cp", None), P("dp", "cp")),
        check_vma=False,
    )
```
